32 devices in a mesh: prompt: 4 (over x, core), sample: 8 (over z, y).
Axes of the slice: x: 2, y: 2, z: 4, core: 2. Of those that a mesh axis runs over, the one named last changes fastest.
Arguments:
- latent: bfloat16 [1024, 576], P('prompt'), may hold values from -16 to 16
- queries: bfloat16 [1024, 128, 576], P('prompt', 'sample'), may hold values from -64 to 64
- cotangent: bfloat16 [1024, 128, 512], P('prompt', 'sample'), may hold values from -18 to 18
- suffix_out: bfloat16 [1024, 128, 512], P('prompt', 'sample'), may hold values from -6 to 6
- suffix_lse: bfloat16 [1024, 128], P('prompt', 'sample'), may hold values from 6 to 10
- rewards: float32 [4], replicated, may hold values from -5 to 5
- slot_sample: int32 [1024], P('prompt'), may hold values from 0 to 4, as said below
Outputs:
- query_grad: bfloat16 [1024, 128, 576], P('prompt', 'sample')
- latent_grad: float32 [1024, 576], P('prompt')
The draws below stay inside these ranges and needn't reach their ends.
Inputs may be any that keep to these rules, and one draw needn't show every extreme that they name: `slot_sample`: on every device the live slots come first and the others hold 4. Read over the devices in order, the live slots' completion numbers never fall, and every completion has a slot. Exactly 512 slots are live in all, and some device has all 256 of its slots live.
All inputs are finite; a program needn't handle non-finite values.
Results may differ from the reference program's by a relative error of at most 0.006.
Values may be sent and summed in bfloat16 or wider, within the bound.
A program may use at most 128 MiB of HBM per device.

```python
import math
import jax
import jax.numpy as jnp
from jax import lax

HEADS = 128
LATENT = 512
ROPE = 64
NOPE = 128
TOK_DEV = 256
PREFIX = 1024
SAMPLES = 4
TOKENS = 1024
N_PROMPT = 4


def prefix_and_queries(key):
    base_key = jax.random.fold_in(key, 101)
    width = LATENT + ROPE
    prefix_rows = jax.random.normal(jax.random.fold_in(base_key, 1), (PREFIX, width), jnp.float32)
    query_rows = 0.55 * jax.random.normal(jax.random.fold_in(base_key, 2), (TOKENS, HEADS, width), jnp.float32)
    return (jnp.clip(prefix_rows, -16.0, 16.0), jnp.clip(query_rows, -64.0, 64.0))


def draw_latent(key, part):
    return prefix_and_queries(key)[0].astype(jnp.bfloat16)


def draw_queries(key, part):
    return prefix_and_queries(key)[1].astype(jnp.bfloat16)


def draw_slot_sample(key, part):
    half_slots = TOK_DEV // 2
    pair_count = N_PROMPT // 2
    shuffled = jax.random.permutation(jax.random.fold_in(key, 11), N_PROMPT)
    shifts = jax.random.randint(jax.random.fold_in(key, 12), (pair_count,), -half_slots, half_slots + 1)
    shifts = shifts.at[0].set(half_slots)
    counts = jnp.zeros((N_PROMPT,), jnp.int32)
    counts = counts.at[shuffled[0::2]].set(half_slots + shifts)
    counts = counts.at[shuffled[1::2]].set(half_slots - shifts)
    live_total = N_PROMPT * half_slots
    boundaries = jnp.sort(jax.random.permutation(jax.random.fold_in(key, 13), live_total - 1)[:SAMPLES - 1] + 1)
    offsets = jnp.cumsum(counts) - counts
    slot_index = jnp.arange(TOK_DEV, dtype=jnp.int32)
    global_rank = offsets[:, None] + slot_index[None, :]
    sample_id = jnp.sum((boundaries[None, None, :] <= global_rank[:, :, None]).astype(jnp.int32), axis=2)
    marked = jnp.where(slot_index[None, :] < counts[:, None], sample_id, SAMPLES)
    return marked.reshape(TOKENS).astype(jnp.int32)


def level_of(key, dims, cuts, low, top_value):
    def one(position, parts):
        steps = jax.random.uniform(jax.random.fold_in(jax.random.fold_in(key, 6), position), (parts,), jnp.float32, low / len(cuts), top_value / len(cuts))
        return jnp.repeat(jnp.exp(steps), dims[position] // parts).reshape((-1,) + (1,) * (len(dims) - position - 1))

    gain = one(*cuts[0])
    for cut in cuts[1:]:
        gain = gain * one(*cut)
    return gain


def scatter_about(own_key, dims, spread, most, cuts=(), held_as=jnp.bfloat16):
    drawn = spread * jax.random.normal(own_key, dims, jnp.float32)
    if cuts:
        drawn = drawn * level_of(own_key, dims, cuts, -0.22, 0.18)
    return jnp.clip(drawn, -most, most).astype(held_as)


def setup_inputs(seed: int = 0) -> dict:
    key_list = jax.random.split(jax.random.key(seed), 8)
    return {
        "latent": draw_latent(jax.random.fold_in(key_list[7], 71), 0),
        "queries": draw_queries(jax.random.fold_in(key_list[7], 71), 0),
        "cotangent": scatter_about(key_list[2], (TOKENS, HEADS, LATENT), 3.0, 18.0, ((0, 4), (1, 8))),
        "suffix_out": scatter_about(key_list[3], (TOKENS, HEADS, LATENT), 1.0, 6.0, ((0, 4), (1, 8))),
        "suffix_lse": jnp.clip(6.0 + 4.0 * jax.random.uniform(key_list[4], (TOKENS, HEADS), jnp.float32) ** level_of(key_list[4], (TOKENS, HEADS), ((0, 4), (1, 8)), -0.2, 0.2), 6.0, 10.0).astype(jnp.bfloat16),
        "rewards": scatter_about(key_list[5], (SAMPLES,), 1.0, 5.0, (), jnp.float32),
        "slot_sample": draw_slot_sample(jax.random.fold_in(key_list[7], 71), 0),
    }


def softmax_scale():
    return (0.1 * math.log(40.0) + 1.0) ** 2 / math.sqrt(NOPE + ROPE)

def advantages(rewards, slot_sample):
    centred = rewards - jnp.mean(rewards)
    advantage_table = jnp.concatenate([centred, jnp.zeros((1,), jnp.float32)])
    sample_ids = jnp.arange(advantage_table.shape[0], dtype=jnp.int32)
    return lax.optimization_barrier(jnp.sum(jnp.where(slot_sample[:, None] == sample_ids[None, :], advantage_table[None, :], 0.0), axis=1))

def reference(latent, queries, cotangent, suffix_out, suffix_lse, rewards, slot_sample):
    factor = softmax_scale()
    weight = advantages(rewards, slot_sample)
    values = latent[:, :LATENT]

    def one_head(running, head_index):
        head_query = lax.dynamic_index_in_dim(queries, head_index, 1, keepdims=False)
        head_cot = lax.dynamic_index_in_dim(cotangent, head_index, 1, keepdims=False)
        head_suffix = lax.dynamic_index_in_dim(suffix_out, head_index, 1, keepdims=False)
        head_lse = lax.dynamic_index_in_dim(suffix_lse, head_index, 1, keepdims=False).astype(jnp.float32)
        scores = factor * jnp.dot(head_query, latent.T, preferred_element_type=jnp.float32)
        row_max = lax.optimization_barrier(jnp.max(scores, axis=1))
        prefix_lse = row_max + jnp.log(lax.optimization_barrier(jnp.sum(jnp.exp(scores - row_max[:, None]), axis=1)))
        joint_max = jnp.maximum(prefix_lse, head_lse)
        total_lse = joint_max + jnp.log(jnp.exp(prefix_lse - joint_max) + jnp.exp(head_lse - joint_max))
        probability = jnp.exp(scores - total_lse[:, None])
        scaled = (weight[:, None] * head_cot.astype(jnp.float32)).astype(jnp.bfloat16)
        prob_grad = jnp.dot(scaled, values.T, preferred_element_type=jnp.float32)
        suffix_dot = lax.optimization_barrier(jnp.sum(scaled.astype(jnp.float32) * head_suffix.astype(jnp.float32), axis=1))
        row_delta = lax.optimization_barrier(jnp.sum(probability * prob_grad, axis=1)) + jnp.exp(head_lse - total_lse) * suffix_dot
        score_grad = (factor * probability * (prob_grad - row_delta[:, None])).astype(jnp.bfloat16)
        head_grad = jnp.dot(score_grad, latent, preferred_element_type=jnp.float32).astype(jnp.bfloat16)
        key_term = jnp.dot(score_grad.T, head_query, preferred_element_type=jnp.float32)
        value_term = jnp.dot(probability.astype(jnp.bfloat16).T, scaled, preferred_element_type=jnp.float32)
        latent_term = key_term + jnp.pad(value_term, ((0, 0), (0, ROPE)))
        return (running + latent_term, head_grad)
    start_sum = jnp.zeros((PREFIX, LATENT + ROPE), jnp.float32)
    running, head_grads = lax.scan(one_head, start_sum, jnp.arange(HEADS, dtype=jnp.int32))
    return (jnp.transpose(head_grads, (1, 0, 2)), running)
```

```python
import functools
import math

import jax
import jax.numpy as jnp
from jax import lax
from jax.experimental import pallas as pl
from jax.experimental.pallas import tpu as pltpu
from jax.sharding import PartitionSpec as P

ROPE = 64
NOPE = 128
LOG2E = math.log2(math.e)


def softmax_scale():
    return (0.1 * math.log(40.0) + 1.0) ** 2 / math.sqrt(NOPE + ROPE)


def nt_dot(a, b):
    return lax.dot_general(a, b, (((1,), (1,)), ((), ())), preferred_element_type=jnp.float32)


def nn_dot(a, b):
    return jnp.dot(a, b, preferred_element_type=jnp.float32)


def attend_kernel(factor, keys_ref, q_ref, scaled_ref, dot_ref, lse_ref, dq_ref, acc_ref, keys_t_ref):
    step = pl.program_id(0)
    value_width = scaled_ref.shape[2]

    @pl.when(step == 0)
    def _():
        acc_ref[...] = jnp.zeros_like(acc_ref)
        keys_t_ref[...] = keys_ref[...].T

    q = q_ref[0]
    scaled = scaled_ref[0]
    suffix_dot = dot_ref[0]
    tail = lse_ref[0] * LOG2E
    scores = nn_dot(keys_ref[...], q) * (factor * LOG2E)
    joint = jnp.maximum(jnp.max(scores, axis=0, keepdims=True), tail)
    e = jnp.exp2(scores - joint)
    tail_e = jnp.exp2(tail - joint)
    inv = 1.0 / (jnp.sum(e, axis=0, keepdims=True) + tail_e)
    prob_grad = nt_dot(keys_ref[:, :value_width], scaled)
    delta = (jnp.sum(e * prob_grad, axis=0, keepdims=True) + tail_e * suffix_dot) * inv
    p = e * inv
    ds = (factor * p * (prob_grad - delta)).astype(jnp.bfloat16)
    weights = p.astype(jnp.bfloat16)
    dq_ref[0] = nn_dot(keys_t_ref[...], ds).astype(jnp.bfloat16)
    acc_ref[...] += nt_dot(ds, q)
    acc_ref[:, :value_width] += nn_dot(weights, scaled)


def attend(keys, queries, scaled, suffix_dot, suffix_lse):
    heads, width, slots = queries.shape
    value_width = scaled.shape[2]
    positions = keys.shape[0]
    return pl.pallas_call(
        functools.partial(attend_kernel, softmax_scale()),
        grid=(heads,),
        out_shape=(
            jax.ShapeDtypeStruct((heads, width, slots), jnp.bfloat16),
            jax.ShapeDtypeStruct((positions, width), jnp.float32),
        ),
        in_specs=[
            pl.BlockSpec((positions, width), lambda i: (0, 0)),
            pl.BlockSpec((1, width, slots), lambda i: (i, 0, 0)),
            pl.BlockSpec((1, slots, value_width), lambda i: (i, 0, 0)),
            pl.BlockSpec((1, 1, slots), lambda i: (i, 0, 0)),
            pl.BlockSpec((1, 1, slots), lambda i: (i, 0, 0)),
        ],
        out_specs=(
            pl.BlockSpec((1, width, slots), lambda i: (i, 0, 0)),
            pl.BlockSpec((positions, width), lambda i: (0, 0)),
        ),
        scratch_shapes=[pltpu.VMEM((width, positions), jnp.bfloat16)],
        compiler_params=pltpu.CompilerParams(vmem_limit_bytes=56 * 1024 * 1024),
        name="attend",
    )(keys, queries, scaled, suffix_dot, suffix_lse)


def on_device(latent, queries, cotangent, suffix_out, suffix_lse, rewards, slot_sample):
    keys = lax.all_gather(latent, "prompt", axis=0, tiled=True)
    centred = rewards - jnp.mean(rewards)
    advantage_table = jnp.concatenate([centred, jnp.zeros((1,), jnp.float32)])
    sample_ids = jnp.arange(advantage_table.shape[0], dtype=jnp.int32)
    weight = jnp.sum(
        jnp.where(slot_sample[:, None] == sample_ids[None, :], advantage_table[None, :], 0.0),
        axis=1,
    )
    scaled = (weight[:, None, None] * cotangent.astype(jnp.float32)).astype(jnp.bfloat16)
    suffix_dot = jnp.sum(scaled.astype(jnp.float32) * suffix_out.astype(jnp.float32), axis=2)
    dq, terms = attend(
        keys,
        jnp.transpose(queries, (1, 2, 0)),
        jnp.transpose(scaled, (1, 0, 2)),
        jnp.transpose(suffix_dot)[:, None, :],
        jnp.transpose(suffix_lse.astype(jnp.float32))[:, None, :],
    )
    owner_sums = lax.psum_scatter(terms, "prompt", scatter_dimension=0, tiled=True)
    return (jnp.transpose(dq, (2, 0, 1)), lax.psum(owner_sums, "sample"))


def solution(mesh):
    in_specs = (
        P("prompt", None),
        P("prompt", "sample", None),
        P("prompt", "sample", None),
        P("prompt", "sample", None),
        P("prompt", "sample"),
        P(),
        P("prompt"),
    )
    out_specs = (P("prompt", "sample", None), P("prompt", None))
    return jax.shard_map(
        on_device, mesh=mesh, in_specs=in_specs, out_specs=out_specs, check_vma=False
    )
```

```python
import functools
import math

import jax
import jax.numpy as jnp
from jax import lax
from jax.experimental import pallas as pl
from jax.experimental.pallas import tpu as pltpu
from jax.sharding import PartitionSpec as P

ROPE = 64
NOPE = 128
LOG2E = math.log2(math.e)


def softmax_scale():
    return (0.1 * math.log(40.0) + 1.0) ** 2 / math.sqrt(NOPE + ROPE)


def nt_dot(a, b):
    return lax.dot_general(a, b, (((1,), (1,)), ((), ())), preferred_element_type=jnp.float32)


def nn_dot(a, b):
    return jnp.dot(a, b, preferred_element_type=jnp.float32)


def attend_kernel(factor, keys_ref, q_ref, scaled_ref, dot_ref, lse_ref, dq_ref, terms_ref, acc_ref, keys_t_ref):
    step = pl.program_id(0)
    value_width = scaled_ref.shape[2]

    @pl.when(step == 0)
    def _():
        acc_ref[...] = jnp.zeros_like(acc_ref)
        keys_t_ref[...] = keys_ref[...].T

    q = q_ref[0]
    scaled = scaled_ref[0]
    suffix_dot = dot_ref[0]
    tail = lse_ref[0] * LOG2E
    scores = nn_dot(keys_ref[...], q) * (factor * LOG2E)
    joint = jnp.maximum(jnp.max(scores, axis=0, keepdims=True), tail)
    e = jnp.exp2(scores - joint)
    tail_e = jnp.exp2(tail - joint)
    inv = 1.0 / (jnp.sum(e, axis=0, keepdims=True) + tail_e)
    prob_grad = nt_dot(keys_ref[:, :value_width], scaled)
    delta = (jnp.sum(e * prob_grad, axis=0, keepdims=True) + tail_e * suffix_dot) * inv
    p = e * inv
    ds = (factor * p * (prob_grad - delta)).astype(jnp.bfloat16)
    weights = p.astype(jnp.bfloat16)
    dq_ref[0] = nn_dot(keys_t_ref[...], ds).astype(jnp.bfloat16)
    acc_ref[...] += nt_dot(ds, q)
    acc_ref[:, :value_width] += nn_dot(weights, scaled)

    @pl.when(step == pl.num_programs(0) - 1)
    def _():
        terms_ref[...] = acc_ref[...].astype(terms_ref.dtype)


def attend(keys, queries, scaled, suffix_dot, suffix_lse, terms_type):
    heads, width, slots = queries.shape
    value_width = scaled.shape[2]
    positions = keys.shape[0]
    return pl.pallas_call(
        functools.partial(attend_kernel, softmax_scale()),
        grid=(heads,),
        out_shape=(
            jax.ShapeDtypeStruct((heads, width, slots), jnp.bfloat16),
            jax.ShapeDtypeStruct((positions, width), terms_type),
        ),
        in_specs=[
            pl.BlockSpec((positions, width), lambda i: (0, 0)),
            pl.BlockSpec((1, width, slots), lambda i: (i, 0, 0)),
            pl.BlockSpec((1, slots, value_width), lambda i: (i, 0, 0)),
            pl.BlockSpec((1, 1, slots), lambda i: (i, 0, 0)),
            pl.BlockSpec((1, 1, slots), lambda i: (i, 0, 0)),
        ],
        out_specs=(
            pl.BlockSpec((1, width, slots), lambda i: (i, 0, 0)),
            pl.BlockSpec((positions, width), lambda i: (0, 0)),
        ),
        scratch_shapes=[
            pltpu.VMEM((positions, width), jnp.float32),
            pltpu.VMEM((width, positions), jnp.bfloat16),
        ],
        compiler_params=pltpu.CompilerParams(vmem_limit_bytes=56 * 1024 * 1024),
        name="attend",
    )(keys, queries, scaled, suffix_dot, suffix_lse)


MESH = pl.DeviceIdType.MESH


def remote(src, dst, send_sem, recv_sem, target):
    return pltpu.make_async_remote_copy(
        src_ref=src, dst_ref=dst, send_sem=send_sem, recv_sem=recv_sem,
        device_id=target, device_id_type=MESH,
    )


def greet(targets):
    barrier = pltpu.get_barrier_semaphore()
    for target in targets:
        pl.semaphore_signal(barrier, inc=1, device_id=target, device_id_type=MESH)
    pl.semaphore_wait(barrier, len(targets))


def prompt_peers(chips):
    me = lax.axis_index("prompt")
    sample = lax.axis_index("sample")
    chip, core = me // 2, me % 2
    sibling = (chip * 2 + 1 - core, sample)
    others = [lax.rem(chip + k, chips) for k in range(1, chips)]
    return me, sample, chip, core, sibling, others


def gather_kernel(chips, block_ref, keys_ref, far_ref, send_sem, recv_sem, pass_send, pass_recv, own_sem):
    me, sample, chip, core, sibling, others = prompt_peers(chips)
    targets = [(other * 2 + core, sample) for other in others]
    greet([sibling] + targets)
    own = pltpu.make_async_copy(block_ref, keys_ref.at[me], own_sem)
    own.start()
    far = []
    for k, target in enumerate(targets):
        copy = remote(block_ref, far_ref.at[k], send_sem.at[k], recv_sem.at[k], target)
        copy.start()
        far.append(copy)
    near = [remote(block_ref, keys_ref.at[me], pass_send.at[0], pass_recv.at[0], sibling)]
    near[0].start()
    kept = []
    for k in range(chips - 1):
        far[k].wait_recv()
        origin = lax.rem(chip - (k + 1) + chips, chips) * 2 + core
        onward = remote(
            far_ref.at[k], keys_ref.at[origin], pass_send.at[k + 1], pass_recv.at[k + 1], sibling
        )
        onward.start()
        near.append(onward)
        keep = pltpu.make_async_copy(far_ref.at[k], keys_ref.at[origin], send_sem.at[chips - 1 + k])
        keep.start()
        kept.append(keep)
    own.wait()
    for copy in far:
        copy.wait_send()
    for copy in kept:
        copy.wait()
    for copy in near:
        copy.wait()


def gather_keys(latent, n_prompt):
    rows, width = latent.shape
    chips = n_prompt // 2
    vmem = pl.BlockSpec(memory_space=pltpu.VMEM)
    dma = pltpu.SemaphoreType.DMA
    keys = pl.pallas_call(
        functools.partial(gather_kernel, chips),
        out_shape=jax.ShapeDtypeStruct((n_prompt, rows, width), latent.dtype),
        in_specs=[vmem],
        out_specs=vmem,
        scratch_shapes=[
            pltpu.VMEM((chips - 1, rows, width), latent.dtype),
            dma((2 * chips - 2,)), dma((chips - 1,)), dma((chips,)), dma((chips,)), dma,
        ],
        compiler_params=pltpu.CompilerParams(collective_id=0, has_side_effects=True),
        name="gather_keys",
    )(latent)
    return keys.reshape(n_prompt * rows, width)


def reduce_kernel(
    chips, samples, terms_ref, out_ref,
    near_ref, stage_ref, far_ref, part_ref, piece_ref, final_ref, full_ref,
    near_send, near_recv, far_send, far_recv, piece_send, piece_recv, full_send, full_recv,
):
    me, sample, chip, core, sibling, others = prompt_peers(chips)
    targets = [(other * 2 + core, sample) for other in others]
    peers = [(me, lax.rem(sample + k, samples)) for k in range(1, samples)]
    greet([sibling] + targets + peers)
    wide = jnp.float32
    narrow = terms_ref.dtype
    order = others + [chip]

    near = []
    for k, other in enumerate(order):
        copy = remote(
            terms_ref.at[other * 2 + 1 - core], near_ref.at[k],
            near_send.at[k], near_recv.at[k], sibling,
        )
        copy.start()
        near.append(copy)
    far = []
    for k, other in enumerate(others):
        near[k].wait_recv()
        stage_ref[k] = (terms_ref[other * 2 + core].astype(wide) + near_ref[k].astype(wide)).astype(narrow)
        copy = remote(stage_ref.at[k], far_ref.at[k], far_send.at[k], far_recv.at[k], targets[k])
        copy.start()
        far.append(copy)
    near[-1].wait_recv()
    total = terms_ref[me].astype(wide) + near_ref[chips - 1].astype(wide)
    for k in range(chips - 1):
        far[k].wait_recv()
        total = total + far_ref[k].astype(wide)
    part_ref[...] = total.reshape(part_ref.shape).astype(narrow)

    pieces = []
    for k, peer in enumerate(peers):
        copy = remote(
            part_ref.at[peer[1]], piece_ref.at[k], piece_send.at[k], piece_recv.at[k], peer
        )
        copy.start()
        pieces.append(copy)
    mine = part_ref[sample].astype(wide)
    for k in range(samples - 1):
        pieces[k].wait_recv()
        mine = mine + piece_ref[k].astype(wide)
    final_ref[...] = mine.astype(narrow)

    spread = []
    for k, peer in enumerate(peers):
        copy = remote(final_ref, full_ref.at[k], full_send.at[k], full_recv.at[k], peer)
        copy.start()
        spread.append(copy)
    out_ref[sample] = final_ref[...].astype(wide)
    for k in range(samples - 1):
        spread[k].wait_recv()
        out_ref[lax.rem(sample - (k + 1) + samples, samples)] = full_ref[k].astype(wide)
    for copy in near + far + pieces + spread:
        copy.wait_send()


def reduce_terms(terms, n_prompt, n_sample):
    positions, width = terms.shape
    rows = positions // n_prompt
    chips = n_prompt // 2
    chunk = rows // n_sample
    vmem = pl.BlockSpec(memory_space=pltpu.VMEM)
    dma = pltpu.SemaphoreType.DMA
    kind = terms.dtype
    out = pl.pallas_call(
        functools.partial(reduce_kernel, chips, n_sample),
        out_shape=jax.ShapeDtypeStruct((n_sample, chunk, width), jnp.float32),
        in_specs=[vmem],
        out_specs=vmem,
        scratch_shapes=[
            pltpu.VMEM((chips, rows, width), kind),
            pltpu.VMEM((chips - 1, rows, width), kind),
            pltpu.VMEM((chips - 1, rows, width), kind),
            pltpu.VMEM((n_sample, chunk, width), kind),
            pltpu.VMEM((n_sample - 1, chunk, width), kind),
            pltpu.VMEM((chunk, width), kind),
            pltpu.VMEM((n_sample - 1, chunk, width), kind),
            dma((chips,)), dma((chips,)), dma((chips - 1,)), dma((chips - 1,)),
            dma((n_sample - 1,)), dma((n_sample - 1,)), dma((n_sample - 1,)), dma((n_sample - 1,)),
        ],
        compiler_params=pltpu.CompilerParams(collective_id=1, has_side_effects=True),
        name="reduce_terms",
    )(terms.reshape(n_prompt, rows, width))
    return out.reshape(rows, width)


def on_device(n_prompt, n_sample, latent, queries, cotangent, suffix_out, suffix_lse, rewards, slot_sample):
    direct = n_prompt % 2 == 0 and n_prompt > 2 and latent.shape[0] % (16 * n_sample) == 0
    if direct:
        keys = gather_keys(latent, n_prompt)
    else:
        keys = lax.all_gather(latent, "prompt", axis=0, tiled=True)
    centred = rewards - jnp.mean(rewards)
    advantage_table = jnp.concatenate([centred, jnp.zeros((1,), jnp.float32)])
    sample_ids = jnp.arange(advantage_table.shape[0], dtype=jnp.int32)
    weight = jnp.sum(
        jnp.where(slot_sample[:, None] == sample_ids[None, :], advantage_table[None, :], 0.0),
        axis=1,
    )
    scaled = (weight[:, None, None] * cotangent.astype(jnp.float32)).astype(jnp.bfloat16)
    suffix_dot = jnp.sum(scaled.astype(jnp.float32) * suffix_out.astype(jnp.float32), axis=2)
    dq, terms = attend(
        keys,
        jnp.transpose(queries, (1, 2, 0)),
        jnp.transpose(scaled, (1, 0, 2)),
        jnp.transpose(suffix_dot)[:, None, :],
        jnp.transpose(suffix_lse.astype(jnp.float32))[:, None, :],
        jnp.bfloat16 if direct else jnp.float32,
    )
    query_grad = jnp.transpose(dq, (2, 0, 1))
    if direct:
        return (query_grad, reduce_terms(terms, n_prompt, n_sample))
    owner_sums = lax.psum_scatter(terms, "prompt", scatter_dimension=0, tiled=True)
    return (query_grad, lax.psum(owner_sums, "sample"))


def solution(mesh):
    in_specs = (
        P("prompt", None),
        P("prompt", "sample", None),
        P("prompt", "sample", None),
        P("prompt", "sample", None),
        P("prompt", "sample"),
        P(),
        P("prompt"),
    )
    out_specs = (P("prompt", "sample", None), P("prompt", None))
    return jax.shard_map(
        functools.partial(on_device, mesh.shape["prompt"], mesh.shape["sample"]),
        mesh=mesh, in_specs=in_specs, out_specs=out_specs, check_vma=False,
    )
```

```python
import functools
import math

import jax
import jax.numpy as jnp
from jax import lax
from jax.experimental import pallas as pl
from jax.experimental.pallas import tpu as pltpu
from jax.sharding import PartitionSpec as P

ROPE = 64
NOPE = 128
LOG2E = math.log2(math.e)


def softmax_scale():
    return (0.1 * math.log(40.0) + 1.0) ** 2 / math.sqrt(NOPE + ROPE)


def nt_dot(a, b):
    return lax.dot_general(a, b, (((1,), (1,)), ((), ())), preferred_element_type=jnp.float32)


def nn_dot(a, b):
    return jnp.dot(a, b, preferred_element_type=jnp.float32)


GROUP = 4


def attend_kernel(factor, count, *refs):
    blocks = refs[:count]
    q_ref, scaled_ref, dot_ref, lse_ref, dq_ref, terms_ref, acc_ref, keys_ref, keys_t_ref = refs[count:]
    step = pl.program_id(0)
    group, slots, value_width = scaled_ref.shape

    @pl.when(step == 0)
    def _():
        acc_ref[...] = jnp.zeros_like(acc_ref)
        for k, block in enumerate(blocks):
            rows = block.shape[0]
            keys_ref[pl.ds(k * rows, rows), :] = block[...]
        keys_t_ref[...] = keys_ref[...].T

    grads, weights, queries = [], [], []
    for h in range(group):
        q = q_ref[h]
        scaled = scaled_ref[h]
        suffix_dot = dot_ref[h]
        tail = lse_ref[h] * LOG2E
        scores = nn_dot(keys_ref[...], q) * (factor * LOG2E)
        prob_grad = nt_dot(keys_ref[:, :value_width], scaled)
        joint = jnp.maximum(jnp.max(scores, axis=0, keepdims=True), tail)
        e = jnp.exp2(scores - joint)
        tail_e = jnp.exp2(tail - joint)
        inv = 1.0 / (jnp.sum(e, axis=0, keepdims=True) + tail_e)
        delta = (jnp.sum(e * prob_grad, axis=0, keepdims=True) + tail_e * suffix_dot) * inv
        p = e * inv
        ds = (factor * p * (prob_grad - delta)).astype(jnp.bfloat16)
        dq_ref[h] = nn_dot(keys_t_ref[...], ds).astype(jnp.bfloat16)
        grads.append(ds)
        weights.append(p.astype(jnp.bfloat16))
        queries.append(q.T)
    joined = jnp.concatenate(grads, axis=1)
    q_rows = jnp.concatenate(queries, axis=0)
    scaled_rows = scaled_ref[...].reshape(group * slots, value_width)
    acc_ref[:, :value_width] += nn_dot(
        jnp.concatenate([joined] + weights, axis=1),
        jnp.concatenate([q_rows[:, :value_width], scaled_rows], axis=0),
    )
    acc_ref[:, value_width:] += nn_dot(joined, q_rows[:, value_width:])

    @pl.when(step == pl.num_programs(0) - 1)
    def _():
        terms_ref[...] = acc_ref[...].astype(terms_ref.dtype)


def attend(blocks, queries, scaled, suffix_dot, suffix_lse, terms_type):
    heads, width, slots = queries.shape
    value_width = scaled.shape[2]
    positions = sum(block.shape[0] for block in blocks)
    group = math.gcd(heads, GROUP)
    return pl.pallas_call(
        functools.partial(attend_kernel, softmax_scale(), len(blocks)),
        grid=(heads // group,),
        out_shape=(
            jax.ShapeDtypeStruct((heads, width, slots), jnp.bfloat16),
            jax.ShapeDtypeStruct((positions, width), terms_type),
        ),
        in_specs=[pl.BlockSpec(block.shape, lambda i: (0, 0)) for block in blocks] + [
            pl.BlockSpec((group, width, slots), lambda i: (i, 0, 0)),
            pl.BlockSpec((group, slots, value_width), lambda i: (i, 0, 0)),
            pl.BlockSpec((group, 1, slots), lambda i: (i, 0, 0)),
            pl.BlockSpec((group, 1, slots), lambda i: (i, 0, 0)),
        ],
        out_specs=(
            pl.BlockSpec((group, width, slots), lambda i: (i, 0, 0)),
            pl.BlockSpec((positions, width), lambda i: (0, 0)),
        ),
        scratch_shapes=[
            pltpu.VMEM((positions, width), jnp.float32),
            pltpu.VMEM((positions, width), jnp.bfloat16),
            pltpu.VMEM((width, positions), jnp.bfloat16),
        ],
        compiler_params=pltpu.CompilerParams(vmem_limit_bytes=56 * 1024 * 1024),
        name="attend",
    )(*blocks, queries, scaled, suffix_dot, suffix_lse)


MESH = pl.DeviceIdType.MESH


def remote(src, dst, send_sem, recv_sem, target):
    return pltpu.make_async_remote_copy(
        src_ref=src, dst_ref=dst, send_sem=send_sem, recv_sem=recv_sem,
        device_id=target, device_id_type=MESH,
    )


def greet(targets):
    barrier = pltpu.get_barrier_semaphore()
    for target in targets:
        pl.semaphore_signal(barrier, inc=1, device_id=target, device_id_type=MESH)
    pl.semaphore_wait(barrier, len(targets))


def prompt_peers(chips):
    me = lax.axis_index("prompt")
    sample = lax.axis_index("sample")
    chip, core = me // 2, me % 2
    sibling = (chip * 2 + 1 - core, sample)
    others = [lax.rem(chip + k, chips) for k in range(1, chips)]
    return me, sample, chip, core, sibling, others


def shifted_keys(latent, n_prompt):
    blocks = [latent]
    for k in range(1, n_prompt):
        shift = [(i, (i + k) % n_prompt) for i in range(n_prompt)]
        blocks.append(lax.ppermute(latent, "prompt", shift))
    return blocks


def reduce_kernel(
    chips, samples, terms_ref, out_ref,
    near_ref, stage_ref, far_ref, part_ref, piece_ref, final_ref, full_ref,
    near_send, near_recv, far_send, far_recv, piece_send, piece_recv, full_send, full_recv,
):
    me, sample, chip, core, sibling, others = prompt_peers(chips)
    targets = [(other * 2 + core, sample) for other in others]
    peers = [(me, lax.rem(sample + k, samples)) for k in range(1, samples)]
    greet([sibling] + targets + peers)
    wide = jnp.float32
    narrow = terms_ref.dtype
    order = others + [chip]

    def place(owner):
        return lax.rem(me - owner + 2 * chips, 2 * chips)

    near = []
    for k, other in enumerate(order):
        copy = remote(
            terms_ref.at[place(other * 2 + 1 - core)], near_ref.at[k],
            near_send.at[k], near_recv.at[k], sibling,
        )
        copy.start()
        near.append(copy)
    far = []
    for k, other in enumerate(others):
        near[k].wait_recv()
        stage_ref[k] = (terms_ref[place(other * 2 + core)].astype(wide) + near_ref[k].astype(wide)).astype(narrow)
        copy = remote(stage_ref.at[k], far_ref.at[k], far_send.at[k], far_recv.at[k], targets[k])
        copy.start()
        far.append(copy)
    near[-1].wait_recv()
    total = terms_ref[0].astype(wide) + near_ref[chips - 1].astype(wide)
    for k in range(chips - 1):
        far[k].wait_recv()
        total = total + far_ref[k].astype(wide)
    part_ref[...] = total.reshape(part_ref.shape).astype(narrow)

    pieces = []
    for k, peer in enumerate(peers):
        copy = remote(
            part_ref.at[peer[1]], piece_ref.at[k], piece_send.at[k], piece_recv.at[k], peer
        )
        copy.start()
        pieces.append(copy)
    mine = part_ref[sample].astype(wide)
    for k in range(samples - 1):
        pieces[k].wait_recv()
        mine = mine + piece_ref[k].astype(wide)
    final_ref[...] = mine.astype(narrow)

    spread = []
    for k, peer in enumerate(peers):
        copy = remote(final_ref, full_ref.at[k], full_send.at[k], full_recv.at[k], peer)
        copy.start()
        spread.append(copy)
    out_ref[sample] = final_ref[...].astype(wide)
    for k in range(samples - 1):
        spread[k].wait_recv()
        out_ref[lax.rem(sample - (k + 1) + samples, samples)] = full_ref[k].astype(wide)
    for copy in near + far + pieces + spread:
        copy.wait_send()


def reduce_terms(terms, n_prompt, n_sample):
    positions, width = terms.shape
    rows = positions // n_prompt
    chips = n_prompt // 2
    chunk = rows // n_sample
    vmem = pl.BlockSpec(memory_space=pltpu.VMEM)
    dma = pltpu.SemaphoreType.DMA
    kind = terms.dtype
    out = pl.pallas_call(
        functools.partial(reduce_kernel, chips, n_sample),
        out_shape=jax.ShapeDtypeStruct((n_sample, chunk, width), jnp.float32),
        in_specs=[vmem],
        out_specs=vmem,
        scratch_shapes=[
            pltpu.VMEM((chips, rows, width), kind),
            pltpu.VMEM((chips - 1, rows, width), kind),
            pltpu.VMEM((chips - 1, rows, width), kind),
            pltpu.VMEM((n_sample, chunk, width), kind),
            pltpu.VMEM((n_sample - 1, chunk, width), kind),
            pltpu.VMEM((chunk, width), kind),
            pltpu.VMEM((n_sample - 1, chunk, width), kind),
            dma((chips,)), dma((chips,)), dma((chips - 1,)), dma((chips - 1,)),
            dma((n_sample - 1,)), dma((n_sample - 1,)), dma((n_sample - 1,)), dma((n_sample - 1,)),
        ],
        compiler_params=pltpu.CompilerParams(collective_id=0, has_side_effects=True),
        name="reduce_terms",
    )(terms.reshape(n_prompt, rows, width))
    return out.reshape(rows, width)


def on_device(n_prompt, n_sample, latent, queries, cotangent, suffix_out, suffix_lse, rewards, slot_sample):
    direct = n_prompt % 2 == 0 and n_prompt > 2 and latent.shape[0] % (16 * n_sample) == 0
    if direct:
        blocks = shifted_keys(latent, n_prompt)
    else:
        blocks = [lax.all_gather(latent, "prompt", axis=0, tiled=True)]
    centred = rewards - jnp.mean(rewards)
    advantage_table = jnp.concatenate([centred, jnp.zeros((1,), jnp.float32)])
    sample_ids = jnp.arange(advantage_table.shape[0], dtype=jnp.int32)
    weight = jnp.sum(
        jnp.where(slot_sample[:, None] == sample_ids[None, :], advantage_table[None, :], 0.0),
        axis=1,
    )
    scaled = (weight[:, None, None] * cotangent.astype(jnp.float32)).astype(jnp.bfloat16)
    suffix_dot = jnp.sum(scaled.astype(jnp.float32) * suffix_out.astype(jnp.float32), axis=2)
    dq, terms = attend(
        blocks,
        jnp.transpose(queries, (1, 2, 0)),
        jnp.transpose(scaled, (1, 0, 2)),
        jnp.transpose(suffix_dot)[:, None, :],
        jnp.transpose(suffix_lse.astype(jnp.float32))[:, None, :],
        jnp.bfloat16 if direct else jnp.float32,
    )
    query_grad = jnp.transpose(dq, (2, 0, 1))
    if direct:
        return (query_grad, reduce_terms(terms, n_prompt, n_sample))
    owner_sums = lax.psum_scatter(terms, "prompt", scatter_dimension=0, tiled=True)
    return (query_grad, lax.psum(owner_sums, "sample"))


def solution(mesh):
    in_specs = (
        P("prompt", None),
        P("prompt", "sample", None),
        P("prompt", "sample", None),
        P("prompt", "sample", None),
        P("prompt", "sample"),
        P(),
        P("prompt"),
    )
    out_specs = (P("prompt", "sample", None), P("prompt", None))
    return jax.shard_map(
        functools.partial(on_device, mesh.shape["prompt"], mesh.shape["sample"]),
        mesh=mesh, in_specs=in_specs, out_specs=out_specs, check_vma=False,
    )
```

```python
import functools
import math

import jax
import jax.numpy as jnp
from jax import lax
from jax.experimental import pallas as pl
from jax.experimental.pallas import tpu as pltpu
from jax.sharding import PartitionSpec as P

ROPE = 64
NOPE = 128
LOG2E = math.log2(math.e)


def softmax_scale():
    return (0.1 * math.log(40.0) + 1.0) ** 2 / math.sqrt(NOPE + ROPE)


def nt_dot(a, b):
    return lax.dot_general(a, b, (((1,), (1,)), ((), ())), preferred_element_type=jnp.float32)


def nn_dot(a, b):
    return jnp.dot(a, b, preferred_element_type=jnp.float32)


GROUP = 4
HALVES = 2


def attend_kernel(factor, count, *refs):
    blocks = refs[:count]
    q_ref, scaled_ref, dot_ref, lse_ref, dq_ref, terms_ref, acc_ref, keys_ref, keys_t_ref = refs[count:]
    step = pl.program_id(0)
    group, slots, value_width = scaled_ref.shape

    @pl.when(step == 0)
    def _():
        acc_ref[...] = jnp.zeros_like(acc_ref)
        for k, block in enumerate(blocks):
            rows = block.shape[0]
            keys_ref[pl.ds(k * rows, rows), :] = block[...]
        keys_t_ref[...] = keys_ref[...].T

    grads, weights, queries = [], [], []
    for h in range(group):
        q = q_ref[h]
        scaled = scaled_ref[h]
        suffix_dot = dot_ref[h]
        tail = lse_ref[h] * LOG2E
        scores = nn_dot(keys_ref[...], q) * (factor * LOG2E)
        prob_grad = nt_dot(keys_ref[:, :value_width], scaled)
        joint = jnp.maximum(jnp.max(scores, axis=0, keepdims=True), tail)
        e = jnp.exp2(scores - joint)
        tail_e = jnp.exp2(tail - joint)
        inv = 1.0 / (jnp.sum(e, axis=0, keepdims=True) + tail_e)
        delta = (jnp.sum(e * prob_grad, axis=0, keepdims=True) + tail_e * suffix_dot) * inv
        p = e * inv
        ds = (factor * p * (prob_grad - delta)).astype(jnp.bfloat16)
        dq_ref[h] = nn_dot(keys_t_ref[...], ds).astype(jnp.bfloat16)
        grads.append(ds)
        weights.append(p.astype(jnp.bfloat16))
        queries.append(q.T)
    joined = jnp.concatenate(grads, axis=1)
    q_rows = jnp.concatenate(queries, axis=0)
    scaled_rows = scaled_ref[...].reshape(group * slots, value_width)
    acc_ref[:, :value_width] += nn_dot(
        jnp.concatenate([joined] + weights, axis=1),
        jnp.concatenate([q_rows[:, :value_width], scaled_rows], axis=0),
    )
    acc_ref[:, value_width:] += nn_dot(joined, q_rows[:, value_width:])

    @pl.when(step == pl.num_programs(0) - 1)
    def _():
        terms_ref[...] = acc_ref[...].astype(terms_ref.dtype)


def attend(blocks, queries, scaled, suffix_dot, suffix_lse, terms_type):
    heads, width, slots = queries.shape
    value_width = scaled.shape[2]
    positions = sum(block.shape[0] for block in blocks)
    group = math.gcd(heads, GROUP)
    return pl.pallas_call(
        functools.partial(attend_kernel, softmax_scale(), len(blocks)),
        grid=(heads // group,),
        out_shape=(
            jax.ShapeDtypeStruct((heads, width, slots), jnp.bfloat16),
            jax.ShapeDtypeStruct((positions, width), terms_type),
        ),
        in_specs=[pl.BlockSpec(block.shape, lambda i: (0, 0)) for block in blocks] + [
            pl.BlockSpec((group, width, slots), lambda i: (i, 0, 0)),
            pl.BlockSpec((group, slots, value_width), lambda i: (i, 0, 0)),
            pl.BlockSpec((group, 1, slots), lambda i: (i, 0, 0)),
            pl.BlockSpec((group, 1, slots), lambda i: (i, 0, 0)),
        ],
        out_specs=(
            pl.BlockSpec((group, width, slots), lambda i: (i, 0, 0)),
            pl.BlockSpec((positions, width), lambda i: (0, 0)),
        ),
        scratch_shapes=[
            pltpu.VMEM((positions, width), jnp.float32),
            pltpu.VMEM((positions, width), jnp.bfloat16),
            pltpu.VMEM((width, positions), jnp.bfloat16),
        ],
        compiler_params=pltpu.CompilerParams(vmem_limit_bytes=56 * 1024 * 1024),
        name="attend",
    )(*blocks, queries, scaled, suffix_dot, suffix_lse)


MESH = pl.DeviceIdType.MESH


def remote(src, dst, send_sem, recv_sem, target):
    return pltpu.make_async_remote_copy(
        src_ref=src, dst_ref=dst, send_sem=send_sem, recv_sem=recv_sem,
        device_id=target, device_id_type=MESH,
    )


def greet(targets):
    barrier = pltpu.get_barrier_semaphore()
    for target in targets:
        pl.semaphore_signal(barrier, inc=1, device_id=target, device_id_type=MESH)
    pl.semaphore_wait(barrier, len(targets))


def prompt_peers(chips):
    me = lax.axis_index("prompt")
    sample = lax.axis_index("sample")
    chip, core = me // 2, me % 2
    sibling = (chip * 2 + 1 - core, sample)
    others = [lax.rem(chip + k, chips) for k in range(1, chips)]
    return me, sample, chip, core, sibling, others


def shifted_keys(latent, n_prompt):
    blocks = [latent]
    for k in range(1, n_prompt):
        shift = [(i, (i + k) % n_prompt) for i in range(n_prompt)]
        blocks.append(lax.ppermute(latent, "prompt", shift))
    return blocks


def reduce_kernel(
    chips, samples, terms_ref, out_ref,
    near_ref, stage_ref, far_ref, part_ref, piece_ref, final_ref, full_ref,
    near_send, near_recv, far_send, far_recv, piece_send, piece_recv, full_send, full_recv,
):
    me, sample, chip, core, sibling, others = prompt_peers(chips)
    targets = [(other * 2 + core, sample) for other in others]
    peers = [(me, lax.rem(sample + k, samples)) for k in range(1, samples)]
    greet([sibling] + targets + peers)
    wide = jnp.float32
    narrow = terms_ref.dtype
    order = others + [chip]

    def place(owner):
        return lax.rem(me - owner + 2 * chips, 2 * chips)

    near = []
    for h in range(HALVES):
        for k, other in enumerate(order):
            i = h * chips + k
            copy = remote(
                terms_ref.at[place(other * 2 + 1 - core), h], near_ref.at[i],
                near_send.at[i], near_recv.at[i], sibling,
            )
            copy.start()
            near.append(copy)
    far = []
    for h in range(HALVES):
        for k, other in enumerate(others):
            i = h * (chips - 1) + k
            near[h * chips + k].wait_recv()
            stage_ref[i] = (
                terms_ref[place(other * 2 + core), h].astype(wide) + near_ref[h * chips + k].astype(wide)
            ).astype(narrow)
            copy = remote(stage_ref.at[i], far_ref.at[i], far_send.at[i], far_recv.at[i], targets[k])
            copy.start()
            far.append(copy)
    pieces = []
    for h in range(HALVES):
        near[h * chips + chips - 1].wait_recv()
        total = terms_ref[0, h].astype(wide) + near_ref[h * chips + chips - 1].astype(wide)
        for k in range(chips - 1):
            i = h * (chips - 1) + k
            far[i].wait_recv()
            total = total + far_ref[i].astype(wide)
        part_ref[h] = total.reshape(part_ref.shape[1:]).astype(narrow)
        for k, peer in enumerate(peers):
            i = h * (samples - 1) + k
            copy = remote(
                part_ref.at[h, peer[1]], piece_ref.at[i], piece_send.at[i], piece_recv.at[i], peer
            )
            copy.start()
            pieces.append(copy)
    spread = []
    for h in range(HALVES):
        mine = part_ref[h, sample].astype(wide)
        for k in range(samples - 1):
            i = h * (samples - 1) + k
            pieces[i].wait_recv()
            mine = mine + piece_ref[i].astype(wide)
        final_ref[h] = mine.astype(narrow)
        for k, peer in enumerate(peers):
            i = h * (samples - 1) + k
            copy = remote(final_ref.at[h], full_ref.at[i], full_send.at[i], full_recv.at[i], peer)
            copy.start()
            spread.append(copy)
    for h in range(HALVES):
        out_ref[h, sample] = final_ref[h].astype(wide)
        for k in range(samples - 1):
            i = h * (samples - 1) + k
            spread[i].wait_recv()
            out_ref[h, lax.rem(sample - (k + 1) + samples, samples)] = full_ref[i].astype(wide)
    for copy in near + far + pieces + spread:
        copy.wait_send()


def reduce_terms(terms, n_prompt, n_sample):
    positions, width = terms.shape
    rows = positions // n_prompt
    chips = n_prompt // 2
    half = rows // HALVES
    chunk = half // n_sample
    near, far, links = HALVES * chips, HALVES * (chips - 1), HALVES * (n_sample - 1)
    vmem = pl.BlockSpec(memory_space=pltpu.VMEM)
    dma = pltpu.SemaphoreType.DMA
    kind = terms.dtype
    out = pl.pallas_call(
        functools.partial(reduce_kernel, chips, n_sample),
        out_shape=jax.ShapeDtypeStruct((HALVES, n_sample, chunk, width), jnp.float32),
        in_specs=[vmem],
        out_specs=vmem,
        scratch_shapes=[
            pltpu.VMEM((near, half, width), kind),
            pltpu.VMEM((far, half, width), kind),
            pltpu.VMEM((far, half, width), kind),
            pltpu.VMEM((HALVES, n_sample, chunk, width), kind),
            pltpu.VMEM((links, chunk, width), kind),
            pltpu.VMEM((HALVES, chunk, width), kind),
            pltpu.VMEM((links, chunk, width), kind),
            dma((near,)), dma((near,)), dma((far,)), dma((far,)),
            dma((links,)), dma((links,)), dma((links,)), dma((links,)),
        ],
        compiler_params=pltpu.CompilerParams(collective_id=0, has_side_effects=True),
        name="reduce_terms",
    )(terms.reshape(n_prompt, HALVES, half, width))
    return out.reshape(rows, width)


def on_device(n_prompt, n_sample, latent, queries, cotangent, suffix_out, suffix_lse, rewards, slot_sample):
    direct = n_prompt % 2 == 0 and n_prompt > 2 and latent.shape[0] % (16 * HALVES * n_sample) == 0
    if direct:
        blocks = shifted_keys(latent, n_prompt)
    else:
        blocks = [lax.all_gather(latent, "prompt", axis=0, tiled=True)]
    centred = rewards - jnp.mean(rewards)
    advantage_table = jnp.concatenate([centred, jnp.zeros((1,), jnp.float32)])
    sample_ids = jnp.arange(advantage_table.shape[0], dtype=jnp.int32)
    weight = jnp.sum(
        jnp.where(slot_sample[:, None] == sample_ids[None, :], advantage_table[None, :], 0.0),
        axis=1,
    )
    scaled = (weight[:, None, None] * cotangent.astype(jnp.float32)).astype(jnp.bfloat16)
    suffix_dot = jnp.sum(scaled.astype(jnp.float32) * suffix_out.astype(jnp.float32), axis=2)
    dq, terms = attend(
        blocks,
        jnp.transpose(queries, (1, 2, 0)),
        jnp.transpose(scaled, (1, 0, 2)),
        jnp.transpose(suffix_dot)[:, None, :],
        jnp.transpose(suffix_lse.astype(jnp.float32))[:, None, :],
        jnp.bfloat16 if direct else jnp.float32,
    )
    query_grad = jnp.transpose(dq, (2, 0, 1))
    if direct:
        return (query_grad, reduce_terms(terms, n_prompt, n_sample))
    owner_sums = lax.psum_scatter(terms, "prompt", scatter_dimension=0, tiled=True)
    return (query_grad, lax.psum(owner_sums, "sample"))


def solution(mesh):
    in_specs = (
        P("prompt", None),
        P("prompt", "sample", None),
        P("prompt", "sample", None),
        P("prompt", "sample", None),
        P("prompt", "sample"),
        P(),
        P("prompt"),
    )
    out_specs = (P("prompt", "sample", None), P("prompt", None))
    return jax.shard_map(
        functools.partial(on_device, mesh.shape["prompt"], mesh.shape["sample"]),
        mesh=mesh, in_specs=in_specs, out_specs=out_specs, check_vma=False,
    )
```
